32 devices in a mesh: row: 4 (over y, core), col: 8 (over z, x).
Axes of the slice: x: 2, y: 2, z: 4, core: 2. Of those that a mesh axis runs over, the one named last changes fastest.
Arguments:
- left_panel: bfloat16 [256, 512, 32], P('col', 'row'), may hold values from -6 to 6
- right_panel: bfloat16 [256, 512, 32], P('row', 'col'), may hold values from -6 to 6
- pair_grad: bfloat16 [512, 512, 128], P('row', 'col'), may hold values from -24 to 24
- out_weight: bfloat16 [1024, 128], replicated, may hold values from -0.1875 to 0.1875
Outputs:
- left_grad: float32 [256, 512, 32], P('col', 'row')
- right_grad: float32 [256, 512, 32], P('row', 'col')
- weight_grad: float32 [1024, 128], replicated
The draws below stay inside these ranges and needn't reach their ends.
All inputs are finite; a program needn't handle non-finite values.
Results may differ from the reference program's by a relative error of at most 0.0033.
Values may be sent and summed in bfloat16 or wider, within the bound.
No kernel may reach another device: no remote copies, remote signals or barrier semaphores. Data moves between devices by JAX's collectives and lax.ppermute only.
A program may use at most 64 MiB of HBM per device.

```python
import jax
import jax.numpy as jnp
from jax import lax

N = 512
S = 256
C = 32
P_SIZE = 128


def block_scale(rng, dims, split, smallest, high):
    def one(axis_at, shards_of):
        steps = jax.random.uniform(jax.random.fold_in(jax.random.fold_in(rng, 6), axis_at), (shards_of,), jnp.float32, smallest / len(split), high / len(split))
        return jnp.repeat(jnp.exp(steps), dims[axis_at] // shards_of).reshape((-1,) + (1,) * (len(dims) - axis_at - 1))

    gain = one(*split[0])
    for cut in split[1:]:
        gain = gain * one(*cut)
    return gain


def scatter_about(own_key, extent, spread, limit, pieces=(), kind=jnp.bfloat16):
    array = spread * jax.random.normal(own_key, extent, jnp.float32)
    if pieces:
        array = array * block_scale(own_key, extent, pieces, -0.22, 0.18)
    return jnp.clip(array, -limit, limit).astype(kind)


def setup_inputs(seed: int = 0) -> dict:
    seeds = jax.random.split(jax.random.key(seed), 5)
    return {
        "left_panel": scatter_about(seeds[0], (S, N, C), 1.0, 6.0, ((0, 8), (1, 4))),
        "right_panel": scatter_about(seeds[1], (S, N, C), 1.0, 6.0, ((0, 4), (1, 8))),
        "pair_grad": scatter_about(seeds[2], (N, N, P_SIZE), 4.0, 24.0, ((0, 4), (1, 8))),
        "out_weight": scatter_about(seeds[3], (C * C, P_SIZE), (C * C) ** -0.5, 0.1875),
    }


def reference(left_panel, right_panel, pair_grad, out_weight):
    block_rows = N // 16
    right_flat = right_panel.reshape(S, N * C)
    weight_t = out_weight.T

    def advance(carried, block_index):
        right_acc, weight_acc = carried
        first_row = (block_index * block_rows).astype(jnp.int32)
        grad_rows = lax.dynamic_slice_in_dim(pair_grad, first_row, block_rows, 0).reshape(block_rows * N, P_SIZE)
        left_rows = lax.dynamic_slice_in_dim(left_panel, first_row, block_rows, 1).reshape(S, block_rows * C)
        expanded = (jnp.dot(grad_rows, weight_t, preferred_element_type=jnp.float32) / S).astype(jnp.bfloat16)
        expanded = expanded.reshape(block_rows, N, C, C).transpose(0, 2, 1, 3).reshape(block_rows * C, N * C)
        left_term = lax.dot_general(right_flat, expanded, (((1,), (1,)), ((), ())), preferred_element_type=jnp.float32)
        right_acc = right_acc + jnp.dot(left_rows, expanded, preferred_element_type=jnp.float32)
        outer_prod = lax.dot_general(left_rows, right_flat, (((0,), (0,)), ((), ())), preferred_element_type=jnp.float32)
        outer_prod = (outer_prod / S).astype(jnp.bfloat16)
        outer_prod = outer_prod.reshape(block_rows, C, N, C).transpose(0, 2, 1, 3).reshape(block_rows * N, C * C)
        weight_acc = weight_acc + lax.dot_general(outer_prod, grad_rows, (((0,), (0,)), ((), ())), preferred_element_type=jnp.float32)
        return (right_acc, weight_acc), left_term

    start_state = (jnp.zeros((S, N * C), jnp.float32), jnp.zeros((C * C, P_SIZE), jnp.float32))
    (right_acc, weight_acc), left_terms = lax.scan(advance, start_state, jnp.arange(16, dtype=jnp.int32))
    left_grad = left_terms.reshape(16, S, block_rows, C).transpose(1, 0, 2, 3).reshape(S, N, C)
    right_grad = right_acc.reshape(S, N, C)
    return left_grad, right_grad, weight_acc / N
```

```python
import functools

import jax
import jax.numpy as jnp
from jax import lax
from jax.experimental import pallas as pl
from jax.experimental.pallas import tpu as pltpu
from jax.sharding import PartitionSpec as P

LANES = 128
BLOCK = 16
BF16 = jnp.bfloat16
F32 = jnp.float32


def cost(flops, moved):
    return pl.CostEstimate(flops=flops, bytes_accessed=moved, transcendentals=0)


def params(mib):
    return pltpu.CompilerParams(vmem_limit_bytes=mib << 20)


def expand_kernel(channels, grad_ref, weight_ref, expanded_ref, turned_ref, wide):
    rows, block, pair_width = grad_ref.shape
    wide[...] = grad_ref[...].astype(F32).reshape(rows * block, pair_width)

    def pair_of_columns(step, carry):
        first = step * 2
        for half in range(2):
            turned_ref[first + half] = wide[pl.ds(first + half, rows, stride=block), :].astype(BF16)
        both = turned_ref[pl.ds(first, 2)].reshape(2 * rows, pair_width)
        product = lax.dot_general(
            weight_ref[...], both, (((1,), (1,)), ((), ())), preferred_element_type=F32
        ).astype(BF16)
        for half in range(2):
            for c1 in range(channels):
                expanded_ref[
                    pl.ds(pl.multiple_of((first + half) * channels, channels), channels), pl.ds(c1 * rows, rows)
                ] = product[c1 * channels : (c1 + 1) * channels, half * rows : (half + 1) * rows]
        return carry

    lax.fori_loop(0, block // 2, pair_of_columns, 0)


def expand(pair_grad, out_weight, channels):
    rows, cols, pair_width = pair_grad.shape
    width = channels * rows
    return pl.pallas_call(
        functools.partial(expand_kernel, channels),
        grid=(cols // BLOCK,),
        in_specs=[
            pl.BlockSpec((rows, BLOCK, pair_width), lambda b: (0, b, 0)),
            pl.BlockSpec(out_weight.shape, lambda b: (0, 0)),
        ],
        out_specs=[
            pl.BlockSpec((BLOCK * channels, width), lambda b: (b, 0)),
            pl.BlockSpec((BLOCK, rows, pair_width), lambda b: (b, 0, 0)),
        ],
        out_shape=[
            jax.ShapeDtypeStruct((cols * channels, width), BF16),
            jax.ShapeDtypeStruct((cols, rows, pair_width), BF16),
        ],
        scratch_shapes=[pltpu.VMEM((rows * BLOCK, pair_width), F32)],
        compiler_params=params(32),
        cost_estimate=cost(2 * rows * cols * channels * channels * pair_width, 2 * cols * channels * width),
        name="expand",
    )(pair_grad, out_weight)


def left_kernel(right_ref, expanded_ref, out_ref):
    out_ref[...] = jnp.dot(right_ref[...], expanded_ref[...], preferred_element_type=F32).astype(out_ref.dtype)


def left_product(right_flat, expanded, dtype):
    sequences, depth = right_flat.shape
    width = expanded.shape[1]
    tile = 512
    return pl.pallas_call(
        left_kernel,
        grid=(width // tile,),
        in_specs=[
            pl.BlockSpec((sequences, depth), lambda n: (0, 0)),
            pl.BlockSpec((depth, tile), lambda n: (0, n)),
        ],
        out_specs=pl.BlockSpec((sequences, tile), lambda n: (0, n)),
        out_shape=jax.ShapeDtypeStruct((sequences, width), dtype),
        compiler_params=params(24),
        cost_estimate=cost(2 * sequences * depth * width, 2 * depth * width),
        name="left",
    )(right_flat, expanded)


def right_kernel(left_ref, expanded_ref, out_ref):
    out_ref[...] = lax.dot_general(
        left_ref[...], expanded_ref[...], (((1,), (1,)), ((), ())), preferred_element_type=F32
    ).astype(out_ref.dtype)


def right_product(left_flat, expanded, dtype):
    sequences, width = left_flat.shape
    depth = expanded.shape[0]
    tile = 256
    return pl.pallas_call(
        right_kernel,
        grid=(depth // tile,),
        in_specs=[
            pl.BlockSpec((sequences, width), lambda n: (0, 0)),
            pl.BlockSpec((tile, width), lambda n: (n, 0)),
        ],
        out_specs=pl.BlockSpec((sequences, tile), lambda n: (0, n)),
        out_shape=jax.ShapeDtypeStruct((sequences, depth), dtype),
        compiler_params=params(24),
        cost_estimate=cost(2 * sequences * depth * width, 2 * depth * width),
        name="right",
    )(left_flat, expanded)


def weight_kernel(channels, left_ref, right_ref, turned_ref, out_ref, outer, right_t):
    block, rows, pair_width = turned_ref.shape
    right_t[...] = right_ref[...].T

    for c1 in range(0, channels, 2):
        product = jnp.dot(
            right_t[...], left_ref[:, pl.ds(c1 * rows, 2 * rows)], preferred_element_type=F32
        ).astype(BF16)
        for half in range(2):
            for j in range(block):
                outer[pl.ds((c1 + half) * channels, channels), pl.ds(j * rows, rows)] = product[
                    j * channels : (j + 1) * channels, half * rows : (half + 1) * rows
                ]
    total = jnp.dot(
        outer[...], turned_ref[...].reshape(block * rows, pair_width), preferred_element_type=F32
    )

    @pl.when(pl.program_id(0) == 0)
    def _():
        out_ref[...] = total

    @pl.when(pl.program_id(0) != 0)
    def _():
        out_ref[...] += total


def weight_product(left_flat, right_flat, turned, channels):
    cols, rows, pair_width = turned.shape
    sequences, width = left_flat.shape
    return pl.pallas_call(
        functools.partial(weight_kernel, channels),
        grid=(cols // BLOCK,),
        in_specs=[
            pl.BlockSpec((sequences, width), lambda b: (0, 0)),
            pl.BlockSpec((sequences, BLOCK * channels), lambda b: (0, b)),
            pl.BlockSpec((BLOCK, rows, pair_width), lambda b: (b, 0, 0)),
        ],
        out_specs=pl.BlockSpec((channels * channels, pair_width), lambda b: (0, 0)),
        out_shape=jax.ShapeDtypeStruct((channels * channels, pair_width), F32),
        scratch_shapes=[
            pltpu.VMEM((channels * channels, BLOCK * rows), BF16),
            pltpu.VMEM((BLOCK * channels, sequences), BF16),
        ],
        compiler_params=params(24),
        cost_estimate=cost(4 * sequences * cols * channels * width, 2 * sequences * width),
        name="weight",
    )(left_flat, right_flat, turned)


def by_tiles(left_panel, right_panel, pair_grad, out_weight):
    left_here, rows, channels = left_panel.shape
    right_here, cols, _ = right_panel.shape
    left_flat = left_panel.transpose(0, 2, 1).reshape(left_here, channels * rows)
    right_flat = right_panel.reshape(right_here, cols * channels)
    left_flat = lax.all_gather(left_flat, "col", axis=0, tiled=True)
    right_flat = lax.all_gather(right_flat, "row", axis=0, tiled=True)
    sequences = left_flat.shape[0]

    expanded, turned = expand(pair_grad, out_weight, channels)
    left_terms = left_product(right_flat, expanded, F32)
    weight_terms = weight_product(left_flat, right_flat, turned, channels)
    right_terms = right_product(left_flat, expanded, F32)

    scale = 1.0 / sequences
    left_grad = lax.psum_scatter(left_terms, "col", scatter_dimension=0, tiled=True) * scale
    left_grad = left_grad.reshape(left_here, channels, rows).transpose(0, 2, 1)
    right_grad = lax.psum_scatter(right_terms, "row", scatter_dimension=0, tiled=True) * scale
    right_grad = right_grad.reshape(right_here, cols, channels)
    residues = rows * lax.axis_size("row")
    weight_grad = lax.psum(weight_terms, ("row", "col")) * (scale / residues)
    return left_grad, right_grad, weight_grad


def by_blocks(left_panel, right_panel, pair_grad, out_weight):
    whole_left = lax.all_gather(left_panel, "col", axis=0, tiled=True)
    whole_right = lax.all_gather(right_panel, "row", axis=0, tiled=True)
    sequences, rows_here, channels = whole_left.shape
    cols_here = whole_right.shape[1]
    pair_width = pair_grad.shape[2]
    residues = rows_here * lax.axis_size("row")
    block_rows = 16
    blocks_total = rows_here // block_rows
    right_flat = whole_right.reshape(sequences, cols_here * channels)
    weight_t = out_weight.T

    def advance(carried, block_index):
        right_acc, weight_acc = carried
        first_row = block_index * block_rows
        grad_rows = lax.dynamic_slice_in_dim(pair_grad, first_row, block_rows, 0).reshape(
            block_rows * cols_here, pair_width
        )
        left_rows = lax.dynamic_slice_in_dim(whole_left, first_row, block_rows, 1).reshape(
            sequences, block_rows * channels
        )
        expanded = (
            jnp.dot(grad_rows, weight_t, preferred_element_type=jnp.float32) / sequences
        ).astype(jnp.bfloat16)
        expanded = (
            expanded.reshape(block_rows, cols_here, channels, channels)
            .transpose(0, 2, 1, 3)
            .reshape(block_rows * channels, cols_here * channels)
        )
        left_term = lax.dot_general(
            right_flat, expanded, (((1,), (1,)), ((), ())), preferred_element_type=jnp.float32
        )
        right_acc = right_acc + jnp.dot(left_rows, expanded, preferred_element_type=jnp.float32)
        outer_prod = lax.dot_general(
            left_rows, right_flat, (((0,), (0,)), ((), ())), preferred_element_type=jnp.float32
        )
        outer_prod = (outer_prod / sequences).astype(jnp.bfloat16)
        outer_prod = (
            outer_prod.reshape(block_rows, channels, cols_here, channels)
            .transpose(0, 2, 1, 3)
            .reshape(block_rows * cols_here, channels * channels)
        )
        weight_acc = weight_acc + lax.dot_general(
            outer_prod, grad_rows, (((0,), (0,)), ((), ())), preferred_element_type=jnp.float32
        )
        return ((right_acc, weight_acc), left_term)

    start_state = (
        jnp.zeros((sequences, cols_here * channels), jnp.float32),
        jnp.zeros(out_weight.shape, jnp.float32),
    )
    (right_acc, weight_acc), left_terms = lax.scan(
        advance, start_state, jnp.arange(blocks_total, dtype=jnp.int32)
    )
    left_terms = lax.psum_scatter(left_terms, "col", scatter_dimension=1, tiled=True)
    left_grad = (
        left_terms.reshape(blocks_total, -1, block_rows, channels)
        .transpose(1, 0, 2, 3)
        .reshape(-1, rows_here, channels)
    )
    right_grad = lax.psum_scatter(right_acc, "row", scatter_dimension=0, tiled=True).reshape(
        -1, cols_here, channels
    )
    weight_total = lax.psum(lax.psum(weight_acc, "col"), "row")
    return (left_grad, right_grad, weight_total / residues)


def per_device(left_panel, right_panel, pair_grad, out_weight):
    rows, cols = pair_grad.shape[:2]
    fits = rows % LANES == 0 and cols % BLOCK == 0
    path = by_tiles if fits else by_blocks
    return path(left_panel, right_panel, pair_grad, out_weight)


def solution(mesh):
    in_specs = (P("col", "row", None), P("row", "col", None), P("row", "col", None), P())
    out_specs = (P("col", "row", None), P("row", "col", None), P())
    return jax.shard_map(
        per_device, mesh=mesh, in_specs=in_specs, out_specs=out_specs, check_vma=False
    )
```

```python
import jax
import jax.numpy as jnp
from jax import lax
from jax.experimental import pallas as pl
from jax.experimental.pallas import tpu as pltpu
from jax.sharding import Mesh
from jax.sharding import PartitionSpec as P

LANES = 128
BLOCK = 16
BF16 = jnp.bfloat16
F32 = jnp.float32


def cost(flops, moved):
    return pl.CostEstimate(flops=flops, bytes_accessed=moved, transcendentals=0)


def params(mib):
    return pltpu.CompilerParams(vmem_limit_bytes=mib << 20)


def toggled(axis, bit):
    return [(i, i ^ bit) for i in range(lax.axis_size(axis))]


def permute(array, axis, bit):
    return lax.ppermute(array, axis, toggled(axis, bit))


def gather(piece, axis):
    pieces = {0: piece}
    for bit in range(2, lax.axis_size(axis), 2):
        pieces[bit] = permute(piece, axis, bit)
    for bit in range(0, lax.axis_size(axis), 2):
        pieces[bit + 1] = permute(pieces[bit], axis, 1)
    return [pieces[bit] for bit in range(lax.axis_size(axis))]


def scatter(slots, axis):
    size = lax.axis_size(axis)
    sums = {}
    for bit in range(0, size, 2):
        near = permute(slots[bit + 1], axis, 1)
        sums[bit] = slots[bit].astype(F32) + near.astype(F32)
    total = sums[0]
    for bit in range(2, size, 2):
        total = total + permute(sums[bit].astype(BF16), axis, bit).astype(F32)
    return total


def reduce_everywhere(whole, scale):
    half = whole.shape[0] // 2
    mine = lax.axis_index("core")
    kept = lax.dynamic_slice_in_dim(whole, mine * half, half, 0)
    sent = lax.dynamic_slice_in_dim(whole, (1 - mine) * half, half, 0)
    kept = kept + permute(sent, "core", 1)
    chips = ("far", "col")
    count = lax.axis_size("far") * lax.axis_size("col")
    parts = lax.all_to_all(kept.reshape(count, half // count, -1), chips, 0, 0, tiled=True)
    part = jnp.sum(parts, axis=0) * scale
    parts = lax.all_to_all(jnp.broadcast_to(part, (count, *part.shape)), chips, 0, 0, tiled=True)
    kept = parts.reshape(half, -1)
    other = permute(kept, "core", 1)
    return jnp.where(mine == 0, jnp.concatenate([kept, other]), jnp.concatenate([other, kept]))


def expand(pair_grad, out_weight, channels, blocks, earlier=()):
    rows, cols, pair_width = pair_grad.shape
    width = channels * rows
    first, count = blocks
    chunk = 8 * channels

    def kernel(*refs):
        grad_ref, weight_ref, *_, expanded_ref, turned_ref, wide = refs
        wide[...] = grad_ref[...].astype(F32).reshape(rows * BLOCK, pair_width)

        def pair_of_columns(step, carry):
            column = step * 2
            for half in range(2):
                turned_ref[column + half] = wide[pl.ds(column + half, rows, stride=BLOCK), :].astype(BF16)
            both = turned_ref[pl.ds(column, 2)].reshape(2 * rows, pair_width)
            for start in range(0, channels * channels, chunk):
                product = lax.dot_general(
                    weight_ref[start : start + chunk, :], both, (((1,), (1,)), ((), ())), preferred_element_type=F32
                ).astype(BF16)
                for half in range(2):
                    row = pl.multiple_of((column + half) * channels, channels)
                    for c1 in range(chunk // channels):
                        expanded_ref[pl.ds(row, channels), pl.ds((start // channels + c1) * rows, rows)] = product[
                            c1 * channels : (c1 + 1) * channels, half * rows : (half + 1) * rows
                        ]
            return carry

        lax.fori_loop(0, BLOCK // 2, pair_of_columns, 0, unroll=2)

    return pl.pallas_call(
        kernel,
        grid=(count,),
        in_specs=[
            pl.BlockSpec((rows, BLOCK, pair_width), lambda b: (0, first + b, 0)),
            pl.BlockSpec(out_weight.shape, lambda b: (0, 0)),
        ]
        + [pl.BlockSpec(memory_space=pl.ANY)] * len(earlier),
        out_specs=[
            pl.BlockSpec((BLOCK * channels, width), lambda b: (first + b, 0)),
            pl.BlockSpec((BLOCK, rows, pair_width), lambda b: (first + b, 0, 0)),
        ],
        out_shape=[
            pltpu.HBM((cols * channels, width), BF16),
            pltpu.HBM((cols, rows, pair_width), BF16),
        ],
        input_output_aliases={2 + n: n for n in range(len(earlier))},
        scratch_shapes=[pltpu.VMEM((rows * BLOCK, pair_width), F32)],
        compiler_params=params(16),
        cost_estimate=cost(
            4 * rows * count * BLOCK * channels * channels * pair_width, 2 * count * BLOCK * channels * width
        ),
        name="expand",
    )(pair_grad, out_weight, *earlier)


def place(pieces, own, target, slot_rows, slot_own):
    rows = pieces[0].shape[0]
    unit = min(rows, slot_rows)
    for bit, piece in enumerate(pieces):
        for part in range(0, rows, unit):
            row = (own ^ bit) * rows + part
            at = ((row // slot_rows) ^ slot_own) * slot_rows + row % slot_rows
            target[pl.ds(pl.multiple_of(at, unit), unit), :] = piece[part : part + unit, :]


def in_hbm(array):
    return pltpu.with_memory_space_constraint(array, pltpu.HBM)


def whole_spec(array):
    return pl.BlockSpec(array.shape, lambda n: (0,) * array.ndim, pipeline_mode=pl.Buffered(1))


def left_product(own, pieces, expanded, slots):
    sequences = pieces[0].shape[0] * len(pieces)
    depth, width = expanded.shape
    tile = 1024

    def kernel(own_ref, *refs):
        piece_refs, expanded_ref = refs[: len(pieces)], refs[len(pieces)]
        outs, panel = refs[len(pieces) + 1 : -1], refs[-1]
        rows = outs[0].shape[0]

        @pl.when(pl.program_id(0) == 0)
        def _():
            place(piece_refs, own_ref[0], panel, rows, own_ref[1])

        product = jnp.dot(panel[...], expanded_ref[...], preferred_element_type=F32)
        for slot, out in enumerate(outs):
            out[...] = product[slot * rows : (slot + 1) * rows, :].astype(out.dtype)

    return pl.pallas_call(
        kernel,
        grid=(width // tile,),
        in_specs=[pl.BlockSpec(memory_space=pltpu.SMEM)]
        + [whole_spec(piece) for piece in pieces]
        + [pl.BlockSpec((depth, tile), lambda n: (0, n))],
        out_specs=[pl.BlockSpec((sequences // slots, tile), lambda n: (0, n))] * slots,
        out_shape=[pltpu.HBM((sequences // slots, width), BF16)] * slots,
        scratch_shapes=[pltpu.VMEM((sequences, depth), BF16)],
        compiler_params=params(18),
        cost_estimate=cost(2 * sequences * depth * width, 2 * depth * width),
        name="left",
    )(own, *pieces, in_hbm(expanded))


def right_product(own, pieces, expanded, slots, after):
    sequences = pieces[0].shape[0] * len(pieces)
    depth, width = expanded.shape
    tile = 512

    def kernel(own_ref, *refs):
        piece_refs, expanded_ref = refs[: len(pieces)], refs[len(pieces)]
        outs, panel = refs[len(pieces) + 2 : -1], refs[-1]
        rows = outs[0].shape[0]

        @pl.when(pl.program_id(0) == 0)
        def _():
            place(piece_refs, own_ref[0], panel, rows, own_ref[1])

        product = lax.dot_general(
            panel[...], expanded_ref[...], (((1,), (1,)), ((), ())), preferred_element_type=F32
        )
        for slot, out in enumerate(outs):
            out[...] = product[slot * rows : (slot + 1) * rows, :].astype(out.dtype)

    return pl.pallas_call(
        kernel,
        grid=(depth // tile,),
        in_specs=[pl.BlockSpec(memory_space=pltpu.SMEM)]
        + [whole_spec(piece) for piece in pieces]
        + [pl.BlockSpec((tile, width), lambda n: (n, 0)), pl.BlockSpec(memory_space=pl.ANY)],
        out_specs=[pl.BlockSpec((sequences // slots, tile), lambda n: (0, n))] * slots,
        out_shape=[pltpu.HBM((sequences // slots, depth), BF16)] * slots,
        scratch_shapes=[pltpu.VMEM((sequences, width), BF16)],
        compiler_params=params(18),
        cost_estimate=cost(2 * sequences * depth * width, 2 * depth * width),
        name="right",
    )(own, *pieces, in_hbm(expanded), after)


def weight_product(own, lefts, rights, turned, channels, after):
    cols, rows, pair_width = turned.shape
    width = lefts[0].shape[1]
    sequences = lefts[0].shape[0] * len(lefts)

    def kernel(own_ref, *refs):
        left_refs, right_refs = refs[: len(lefts)], refs[len(lefts) : len(lefts) + len(rights)]
        turned_ref, _, out_ref, left, right, right_t, outer = refs[len(lefts) + len(rights) :]
        step = pl.program_id(0)

        @pl.when(step == 0)
        def _():
            place(left_refs, own_ref[1], left, sequences, 0)

        place(right_refs, own_ref[0], right, sequences, 0)
        right_t[...] = right[...].T
        for c1 in range(0, channels, 2):
            product = jnp.dot(
                right_t[...], left[:, c1 * rows : (c1 + 2) * rows], preferred_element_type=F32
            ).astype(BF16)
            for half in range(2):
                for j in range(BLOCK):
                    outer[pl.ds((c1 + half) * channels, channels), pl.ds(j * rows, rows)] = product[
                        j * channels : (j + 1) * channels, half * rows : (half + 1) * rows
                    ]
        total = jnp.dot(
            outer[...], turned_ref[...].reshape(BLOCK * rows, pair_width), preferred_element_type=F32
        )

        @pl.when(step == 0)
        def _():
            out_ref[...] = total

        @pl.when(step != 0)
        def _():
            out_ref[...] += total

    block = BLOCK * channels
    return pl.pallas_call(
        kernel,
        grid=(cols // BLOCK,),
        in_specs=[pl.BlockSpec(memory_space=pltpu.SMEM)]
        + [whole_spec(piece) for piece in lefts]
        + [pl.BlockSpec((piece.shape[0], block), lambda b: (0, b)) for piece in rights]
        + [pl.BlockSpec((BLOCK, rows, pair_width), lambda b: (b, 0, 0)), pl.BlockSpec(memory_space=pl.ANY)],
        out_specs=pl.BlockSpec((channels * channels, pair_width), lambda b: (0, 0)),
        out_shape=jax.ShapeDtypeStruct((channels * channels, pair_width), F32),
        scratch_shapes=[
            pltpu.VMEM((sequences, width), BF16),
            pltpu.VMEM((sequences, block), BF16),
            pltpu.VMEM((block, sequences), BF16),
            pltpu.VMEM((channels * channels, BLOCK * rows), BF16),
        ],
        compiler_params=params(18),
        cost_estimate=cost(4 * sequences * cols * channels * width, 2 * sequences * width),
        name="weight",
    )(own, *lefts, *rights, turned, after)


def by_tiles(left_panel, right_panel, pair_grad, out_weight):
    return tile_plan(left_panel, right_panel, pair_grad, out_weight)


def tile_plan(left_panel, right_panel, pair_grad, out_weight):
    left_here, rows, channels = left_panel.shape
    right_here, cols, _ = right_panel.shape
    split_row = ("far", "core")
    own = jnp.stack([lax.axis_index(split_row), lax.axis_index("col")]).astype(jnp.int32)
    left_flat = left_panel.transpose(0, 2, 1).reshape(left_here, channels * rows)
    right_flat = right_panel.reshape(right_here, cols * channels)
    lefts = gather(left_flat, "col")
    rights = gather(right_flat, split_row)
    sequences = left_here * len(lefts)
    scale = 1.0 / sequences

    lefts, rights = [in_hbm(piece) for piece in lefts], [in_hbm(piece) for piece in rights]
    pair_grad, out_weight = in_hbm(pair_grad), in_hbm(out_weight)
    blocks = cols // BLOCK
    early = blocks // 2
    arrays = ()
    if early:
        arrays = expand(pair_grad, out_weight, channels, (0, early))
    expanded, turned = expand(pair_grad, out_weight, channels, (early, blocks - early), arrays)
    left_slots = left_product(own, rights, expanded, len(lefts))
    weight_terms = weight_product(own, lefts, rights, turned, channels, left_slots[0])
    right_slots = right_product(own[::-1], lefts, expanded, len(rights), weight_terms)

    left_grad = scatter(left_slots, "col") * scale
    left_grad = left_grad.reshape(left_here, channels, rows).transpose(0, 2, 1)
    right_grad = scatter(right_slots, split_row) * scale
    right_grad = right_grad.reshape(right_here, cols, channels)
    residues = rows * lax.axis_size(split_row)
    weight_grad = reduce_everywhere(weight_terms, scale / residues)
    return left_grad, right_grad, weight_grad


def by_blocks(left_panel, right_panel, pair_grad, out_weight):
    whole_left = lax.all_gather(left_panel, "col", axis=0, tiled=True)
    whole_right = lax.all_gather(right_panel, "row", axis=0, tiled=True)
    sequences, rows_here, channels = whole_left.shape
    cols_here = whole_right.shape[1]
    pair_width = pair_grad.shape[2]
    residues = rows_here * lax.axis_size("row")
    block_rows = 16
    blocks_total = rows_here // block_rows
    right_flat = whole_right.reshape(sequences, cols_here * channels)
    weight_t = out_weight.T

    def advance(carried, block_index):
        right_acc, weight_acc = carried
        first_row = block_index * block_rows
        grad_rows = lax.dynamic_slice_in_dim(pair_grad, first_row, block_rows, 0).reshape(
            block_rows * cols_here, pair_width
        )
        left_rows = lax.dynamic_slice_in_dim(whole_left, first_row, block_rows, 1).reshape(
            sequences, block_rows * channels
        )
        expanded = (
            jnp.dot(grad_rows, weight_t, preferred_element_type=jnp.float32) / sequences
        ).astype(jnp.bfloat16)
        expanded = (
            expanded.reshape(block_rows, cols_here, channels, channels)
            .transpose(0, 2, 1, 3)
            .reshape(block_rows * channels, cols_here * channels)
        )
        left_term = lax.dot_general(
            right_flat, expanded, (((1,), (1,)), ((), ())), preferred_element_type=jnp.float32
        )
        right_acc = right_acc + jnp.dot(left_rows, expanded, preferred_element_type=jnp.float32)
        outer_prod = lax.dot_general(
            left_rows, right_flat, (((0,), (0,)), ((), ())), preferred_element_type=jnp.float32
        )
        outer_prod = (outer_prod / sequences).astype(jnp.bfloat16)
        outer_prod = (
            outer_prod.reshape(block_rows, channels, cols_here, channels)
            .transpose(0, 2, 1, 3)
            .reshape(block_rows * cols_here, channels * channels)
        )
        weight_acc = weight_acc + lax.dot_general(
            outer_prod, grad_rows, (((0,), (0,)), ((), ())), preferred_element_type=jnp.float32
        )
        return ((right_acc, weight_acc), left_term)

    start_state = (
        jnp.zeros((sequences, cols_here * channels), jnp.float32),
        jnp.zeros(out_weight.shape, jnp.float32),
    )
    (right_acc, weight_acc), left_terms = lax.scan(
        advance, start_state, jnp.arange(blocks_total, dtype=jnp.int32)
    )
    left_terms = lax.psum_scatter(left_terms, "col", scatter_dimension=1, tiled=True)
    left_grad = (
        left_terms.reshape(blocks_total, -1, block_rows, channels)
        .transpose(1, 0, 2, 3)
        .reshape(-1, rows_here, channels)
    )
    right_grad = lax.psum_scatter(right_acc, "row", scatter_dimension=0, tiled=True).reshape(
        -1, cols_here, channels
    )
    weight_total = lax.psum(lax.psum(weight_acc, "col"), "row")
    return (left_grad, right_grad, weight_total / residues)


def powers_of_two(*sizes):
    return all(size > 1 and size & (size - 1) == 0 for size in sizes)


def solution(mesh):
    def run(left_panel, right_panel, pair_grad, out_weight):
        n_row, n_col = mesh.shape["row"], mesh.shape["col"]
        rows, cols = pair_grad.shape[0] // n_row, pair_grad.shape[1] // n_col
        tiles = rows == LANES and cols % BLOCK == 0 and powers_of_two(n_row, n_col)
        if tiles:
            devices = mesh.devices.reshape(n_row // 2, 2, n_col)
            used, row, body = Mesh(devices, ("far", "core", "col")), ("far", "core"), by_tiles
        else:
            used, row, body = mesh, "row", by_blocks
        return jax.shard_map(
            body,
            mesh=used,
            in_specs=(P("col", row, None), P(row, "col", None), P(row, "col", None), P()),
            out_specs=(P("col", row, None), P(row, "col", None), P()),
            check_vma=False,
        )(left_panel, right_panel, pair_grad, out_weight)

    return run
```

```python
import jax
import jax.numpy as jnp
from jax import lax
from jax.experimental import pallas as pl
from jax.experimental.pallas import tpu as pltpu
from jax.sharding import Mesh
from jax.sharding import PartitionSpec as P

LANES = 128
BLOCK = 16
BF16 = jnp.bfloat16
F32 = jnp.float32


def cost(flops, moved):
    return pl.CostEstimate(flops=flops, bytes_accessed=moved, transcendentals=0)


def params(mib):
    return pltpu.CompilerParams(vmem_limit_bytes=mib << 20)


def toggled(axis, bit):
    return [(i, i ^ bit) for i in range(lax.axis_size(axis))]


def permute(array, axis, bit):
    return lax.ppermute(array, axis, toggled(axis, bit))


def gather(piece, axis):
    pieces = {0: piece}
    for bit in range(2, lax.axis_size(axis), 2):
        pieces[bit] = permute(piece, axis, bit)
    for bit in range(0, lax.axis_size(axis), 2):
        pieces[bit + 1] = permute(pieces[bit], axis, 1)
    return [pieces[bit] for bit in range(lax.axis_size(axis))]


def scatter(slots, axis):
    size = lax.axis_size(axis)
    sums = {}
    for bit in range(0, size, 2):
        near = permute(slots[bit + 1], axis, 1)
        sums[bit] = slots[bit].astype(F32) + near.astype(F32)
    total = sums[0]
    for bit in range(2, size, 2):
        total = total + permute(sums[bit].astype(BF16), axis, bit).astype(F32)
    return total


def reduce_everywhere(whole, scale):
    half = whole.shape[0] // 2
    mine = lax.axis_index("core")
    kept = lax.dynamic_slice_in_dim(whole, mine * half, half, 0)
    sent = lax.dynamic_slice_in_dim(whole, (1 - mine) * half, half, 0)
    kept = kept + permute(sent, "core", 1)
    chips = ("far", "col")
    count = lax.axis_size("far") * lax.axis_size("col")
    parts = lax.all_to_all(kept.reshape(count, half // count, -1), chips, 0, 0, tiled=True)
    part = jnp.sum(parts, axis=0) * scale
    parts = lax.all_to_all(jnp.broadcast_to(part, (count, *part.shape)), chips, 0, 0, tiled=True)
    kept = parts.reshape(half, -1)
    other = permute(kept, "core", 1)
    return jnp.where(mine == 0, jnp.concatenate([kept, other]), jnp.concatenate([other, kept]))


def expand(pair_grad, out_weight, channels, blocks, earlier=()):
    rows, cols, pair_width = pair_grad.shape
    width = channels * rows
    first, count = blocks
    chunk = 8 * channels

    def kernel(*refs):
        grad_ref, weight_ref, *_, expanded_ref, turned_ref, wide = refs
        wide[...] = grad_ref[...].astype(F32).reshape(rows * BLOCK, pair_width)

        def pair_of_columns(step, carry):
            column = step * 2
            for half in range(2):
                turned_ref[column + half] = wide[pl.ds(column + half, rows, stride=BLOCK), :].astype(BF16)
            both = turned_ref[pl.ds(column, 2)].reshape(2 * rows, pair_width)
            for start in range(0, channels * channels, chunk):
                product = lax.dot_general(
                    weight_ref[start : start + chunk, :], both, (((1,), (1,)), ((), ())), preferred_element_type=F32
                ).astype(BF16)
                for half in range(2):
                    row = pl.multiple_of((column + half) * channels, channels)
                    for c1 in range(chunk // channels):
                        expanded_ref[pl.ds(row, channels), pl.ds((start // channels + c1) * rows, rows)] = product[
                            c1 * channels : (c1 + 1) * channels, half * rows : (half + 1) * rows
                        ]
            return carry

        lax.fori_loop(0, BLOCK // 2, pair_of_columns, 0, unroll=2)

    return pl.pallas_call(
        kernel,
        grid=(count,),
        in_specs=[
            pl.BlockSpec((rows, BLOCK, pair_width), lambda b: (0, first + b, 0)),
            pl.BlockSpec(out_weight.shape, lambda b: (0, 0)),
        ]
        + [pl.BlockSpec(memory_space=pl.ANY)] * len(earlier),
        out_specs=[
            pl.BlockSpec((BLOCK * channels, width), lambda b: (first + b, 0)),
            pl.BlockSpec((BLOCK, rows, pair_width), lambda b: (first + b, 0, 0)),
        ],
        out_shape=[
            pltpu.HBM((cols * channels, width), BF16),
            pltpu.HBM((cols, rows, pair_width), BF16),
        ],
        input_output_aliases={2 + n: n for n in range(len(earlier))},
        scratch_shapes=[pltpu.VMEM((rows * BLOCK, pair_width), F32)],
        compiler_params=params(16),
        cost_estimate=cost(
            4 * rows * count * BLOCK * channels * channels * pair_width, 2 * count * BLOCK * channels * width
        ),
        name="expand",
    )(pair_grad, out_weight, *earlier)


def place(pieces, own, target, slot_rows, slot_own):
    rows = pieces[0].shape[0]
    unit = min(rows, slot_rows)
    for bit, piece in enumerate(pieces):
        for part in range(0, rows, unit):
            row = (own ^ bit) * rows + part
            at = ((row // slot_rows) ^ slot_own) * slot_rows + row % slot_rows
            target[pl.ds(pl.multiple_of(at, unit), unit), :] = piece[part : part + unit, :]


def in_hbm(array):
    return pltpu.with_memory_space_constraint(array, pltpu.HBM)


def whole_spec(array):
    return pl.BlockSpec(array.shape, lambda n: (0,) * array.ndim, pipeline_mode=pl.Buffered(1))


def left_product(own, pieces, expanded, slots):
    sequences = pieces[0].shape[0] * len(pieces)
    depth, width = expanded.shape
    tile = 1024

    def kernel(own_ref, *refs):
        piece_refs, expanded_ref = refs[: len(pieces)], refs[len(pieces)]
        outs, panel = refs[len(pieces) + 1 : -1], refs[-1]
        rows = outs[0].shape[0]

        @pl.when(pl.program_id(0) == 0)
        def _():
            place(piece_refs, own_ref[0], panel, rows, own_ref[1])

        product = jnp.dot(panel[...], expanded_ref[...], preferred_element_type=F32)
        for slot, out in enumerate(outs):
            out[...] = product[slot * rows : (slot + 1) * rows, :].astype(out.dtype)

    return pl.pallas_call(
        kernel,
        grid=(width // tile,),
        in_specs=[pl.BlockSpec(memory_space=pltpu.SMEM)]
        + [whole_spec(piece) for piece in pieces]
        + [pl.BlockSpec((depth, tile), lambda n: (0, n))],
        out_specs=[pl.BlockSpec((sequences // slots, tile), lambda n: (0, n))] * slots,
        out_shape=[pltpu.HBM((sequences // slots, width), BF16)] * slots,
        scratch_shapes=[pltpu.VMEM((sequences, depth), BF16)],
        compiler_params=params(18),
        cost_estimate=cost(2 * sequences * depth * width, 2 * depth * width),
        name="left",
    )(own, *pieces, in_hbm(expanded))


def right_product(own, pieces, expanded, slots, after):
    sequences = pieces[0].shape[0] * len(pieces)
    depth, width = expanded.shape
    tile = 512

    def kernel(own_ref, *refs):
        piece_refs, expanded_ref = refs[: len(pieces)], refs[len(pieces)]
        outs, panel = refs[len(pieces) + 2 : -1], refs[-1]
        rows = outs[0].shape[0]

        @pl.when(pl.program_id(0) == 0)
        def _():
            place(piece_refs, own_ref[0], panel, rows, own_ref[1])

        product = lax.dot_general(
            panel[...], expanded_ref[...], (((1,), (1,)), ((), ())), preferred_element_type=F32
        )
        for slot, out in enumerate(outs):
            out[...] = product[slot * rows : (slot + 1) * rows, :].astype(out.dtype)

    return pl.pallas_call(
        kernel,
        grid=(depth // tile,),
        in_specs=[pl.BlockSpec(memory_space=pltpu.SMEM)]
        + [whole_spec(piece) for piece in pieces]
        + [pl.BlockSpec((tile, width), lambda n: (n, 0)), pl.BlockSpec(memory_space=pl.ANY)],
        out_specs=[pl.BlockSpec((sequences // slots, tile), lambda n: (0, n))] * slots,
        out_shape=[pltpu.HBM((sequences // slots, depth), BF16)] * slots,
        scratch_shapes=[pltpu.VMEM((sequences, width), BF16)],
        compiler_params=params(18),
        cost_estimate=cost(2 * sequences * depth * width, 2 * depth * width),
        name="right",
    )(own, *pieces, in_hbm(expanded), after)


def weight_product(own, lefts, rights, turned, channels, after, blocks, earlier=()):
    first, count = blocks
    _, rows, pair_width = turned.shape
    width = lefts[0].shape[1]
    sequences = lefts[0].shape[0] * len(lefts)

    def kernel(own_ref, *refs):
        left_refs, right_refs = refs[: len(lefts)], refs[len(lefts) : len(lefts) + len(rights)]
        turned_ref, _, *earlier_refs = refs[len(lefts) + len(rights) : -5]
        out_ref, left, right, right_t, outer = refs[-5:]
        step = pl.program_id(0)

        @pl.when(step == 0)
        def _():
            place(left_refs, own_ref[1], left, sequences, 0)

        place(right_refs, own_ref[0], right, sequences, 0)
        right_t[...] = right[...].T
        for c1 in range(0, channels, 2):
            product = jnp.dot(
                right_t[...], left[:, c1 * rows : (c1 + 2) * rows], preferred_element_type=F32
            ).astype(BF16)
            for half in range(2):
                for j in range(BLOCK):
                    outer[pl.ds((c1 + half) * channels, channels), pl.ds(j * rows, rows)] = product[
                        j * channels : (j + 1) * channels, half * rows : (half + 1) * rows
                    ]
        total = jnp.dot(
            outer[...], turned_ref[...].reshape(BLOCK * rows, pair_width), preferred_element_type=F32
        )

        @pl.when(step == 0)
        def _():
            out_ref[...] = total + earlier_refs[0][...] if earlier else total

        @pl.when(step != 0)
        def _():
            out_ref[...] += total

    block = BLOCK * channels
    return pl.pallas_call(
        kernel,
        grid=(count,),
        in_specs=[pl.BlockSpec(memory_space=pltpu.SMEM)]
        + [whole_spec(piece) for piece in lefts]
        + [pl.BlockSpec((piece.shape[0], block), lambda b: (0, first + b)) for piece in rights]
        + [pl.BlockSpec((BLOCK, rows, pair_width), lambda b: (first + b, 0, 0)), pl.BlockSpec(memory_space=pl.ANY)]
        + [whole_spec(array) for array in earlier],
        out_specs=pl.BlockSpec((channels * channels, pair_width), lambda b: (0, 0)),
        out_shape=jax.ShapeDtypeStruct((channels * channels, pair_width), F32),
        scratch_shapes=[
            pltpu.VMEM((sequences, width), BF16),
            pltpu.VMEM((sequences, block), BF16),
            pltpu.VMEM((block, sequences), BF16),
            pltpu.VMEM((channels * channels, BLOCK * rows), BF16),
        ],
        compiler_params=params(18),
        cost_estimate=cost(6 * sequences * count * BLOCK * channels * width, 2 * sequences * width),
        name="weight",
    )(own, *lefts, *rights, turned, after, *earlier)


def by_tiles(left_panel, right_panel, pair_grad, out_weight):
    return tile_plan(left_panel, right_panel, pair_grad, out_weight)


def tile_plan(left_panel, right_panel, pair_grad, out_weight):
    left_here, rows, channels = left_panel.shape
    right_here, cols, _ = right_panel.shape
    split_row = ("far", "core")
    own = jnp.stack([lax.axis_index(split_row), lax.axis_index("col")]).astype(jnp.int32)
    left_flat = left_panel.transpose(0, 2, 1).reshape(left_here, channels * rows)
    right_flat = right_panel.reshape(right_here, cols * channels)
    lefts = gather(left_flat, "col")
    rights = gather(right_flat, split_row)
    sequences = left_here * len(lefts)
    scale = 1.0 / sequences

    lefts, rights = [in_hbm(piece) for piece in lefts], [in_hbm(piece) for piece in rights]
    pair_grad, out_weight = in_hbm(pair_grad), in_hbm(out_weight)
    blocks = cols // BLOCK
    early = blocks // 2
    arrays = ()
    if early:
        arrays = expand(pair_grad, out_weight, channels, (0, early))
    expanded, turned = expand(pair_grad, out_weight, channels, (early, blocks - early), arrays)
    left_slots = left_product(own, rights, expanded, len(lefts))
    weight_terms, after = (), left_slots[0]
    for part in ((0, early), (early, blocks - early)):
        if part[1]:
            after = weight_product(own, lefts, rights, turned, channels, after, part, weight_terms)
            weight_terms = (after,)
    weight_terms = after
    right_slots = right_product(own[::-1], lefts, expanded, len(rights), weight_terms)

    left_grad = scatter(left_slots, "col") * scale
    left_grad = left_grad.reshape(left_here, channels, rows).transpose(0, 2, 1)
    right_grad = scatter(right_slots, split_row) * scale
    right_grad = right_grad.reshape(right_here, cols, channels)
    residues = rows * lax.axis_size(split_row)
    weight_grad = reduce_everywhere(weight_terms, scale / residues)
    return left_grad, right_grad, weight_grad


def by_blocks(left_panel, right_panel, pair_grad, out_weight):
    whole_left = lax.all_gather(left_panel, "col", axis=0, tiled=True)
    whole_right = lax.all_gather(right_panel, "row", axis=0, tiled=True)
    sequences, rows_here, channels = whole_left.shape
    cols_here = whole_right.shape[1]
    pair_width = pair_grad.shape[2]
    residues = rows_here * lax.axis_size("row")
    block_rows = 16
    blocks_total = rows_here // block_rows
    right_flat = whole_right.reshape(sequences, cols_here * channels)
    weight_t = out_weight.T

    def advance(carried, block_index):
        right_acc, weight_acc = carried
        first_row = block_index * block_rows
        grad_rows = lax.dynamic_slice_in_dim(pair_grad, first_row, block_rows, 0).reshape(
            block_rows * cols_here, pair_width
        )
        left_rows = lax.dynamic_slice_in_dim(whole_left, first_row, block_rows, 1).reshape(
            sequences, block_rows * channels
        )
        expanded = (
            jnp.dot(grad_rows, weight_t, preferred_element_type=jnp.float32) / sequences
        ).astype(jnp.bfloat16)
        expanded = (
            expanded.reshape(block_rows, cols_here, channels, channels)
            .transpose(0, 2, 1, 3)
            .reshape(block_rows * channels, cols_here * channels)
        )
        left_term = lax.dot_general(
            right_flat, expanded, (((1,), (1,)), ((), ())), preferred_element_type=jnp.float32
        )
        right_acc = right_acc + jnp.dot(left_rows, expanded, preferred_element_type=jnp.float32)
        outer_prod = lax.dot_general(
            left_rows, right_flat, (((0,), (0,)), ((), ())), preferred_element_type=jnp.float32
        )
        outer_prod = (outer_prod / sequences).astype(jnp.bfloat16)
        outer_prod = (
            outer_prod.reshape(block_rows, channels, cols_here, channels)
            .transpose(0, 2, 1, 3)
            .reshape(block_rows * cols_here, channels * channels)
        )
        weight_acc = weight_acc + lax.dot_general(
            outer_prod, grad_rows, (((0,), (0,)), ((), ())), preferred_element_type=jnp.float32
        )
        return ((right_acc, weight_acc), left_term)

    start_state = (
        jnp.zeros((sequences, cols_here * channels), jnp.float32),
        jnp.zeros(out_weight.shape, jnp.float32),
    )
    (right_acc, weight_acc), left_terms = lax.scan(
        advance, start_state, jnp.arange(blocks_total, dtype=jnp.int32)
    )
    left_terms = lax.psum_scatter(left_terms, "col", scatter_dimension=1, tiled=True)
    left_grad = (
        left_terms.reshape(blocks_total, -1, block_rows, channels)
        .transpose(1, 0, 2, 3)
        .reshape(-1, rows_here, channels)
    )
    right_grad = lax.psum_scatter(right_acc, "row", scatter_dimension=0, tiled=True).reshape(
        -1, cols_here, channels
    )
    weight_total = lax.psum(lax.psum(weight_acc, "col"), "row")
    return (left_grad, right_grad, weight_total / residues)


def powers_of_two(*sizes):
    return all(size > 1 and size & (size - 1) == 0 for size in sizes)


def solution(mesh):
    def run(left_panel, right_panel, pair_grad, out_weight):
        n_row, n_col = mesh.shape["row"], mesh.shape["col"]
        rows, cols = pair_grad.shape[0] // n_row, pair_grad.shape[1] // n_col
        tiles = rows == LANES and cols % BLOCK == 0 and powers_of_two(n_row, n_col)
        if tiles:
            devices = mesh.devices.reshape(n_row // 2, 2, n_col)
            used, row, body = Mesh(devices, ("far", "core", "col")), ("far", "core"), by_tiles
        else:
            used, row, body = mesh, "row", by_blocks
        return jax.shard_map(
            body,
            mesh=used,
            in_specs=(P("col", row, None), P(row, "col", None), P(row, "col", None), P()),
            out_specs=(P("col", row, None), P(row, "col", None), P()),
            check_vma=False,
        )(left_panel, right_panel, pair_grad, out_weight)

    return run
```

```python
import jax
import jax.numpy as jnp
from jax import lax
from jax.experimental import pallas as pl
from jax.experimental.pallas import tpu as pltpu
from jax.sharding import Mesh
from jax.sharding import PartitionSpec as P

LANES = 128
BLOCK = 16
BF16 = jnp.bfloat16
F32 = jnp.float32


def cost(flops, moved):
    return pl.CostEstimate(flops=flops, bytes_accessed=moved, transcendentals=0)


def params(mib):
    return pltpu.CompilerParams(vmem_limit_bytes=mib << 20)


def toggled(axis, bit):
    return [(i, i ^ bit) for i in range(lax.axis_size(axis))]


def permute(array, axis, bit):
    return lax.ppermute(array, axis, toggled(axis, bit))


def gather(piece, axis):
    pieces = {0: piece}
    for bit in range(2, lax.axis_size(axis), 2):
        pieces[bit] = permute(piece, axis, bit)
    for bit in range(0, lax.axis_size(axis), 2):
        pieces[bit + 1] = permute(pieces[bit], axis, 1)
    return [pieces[bit] for bit in range(lax.axis_size(axis))]


def scatter(slots, axis):
    size = lax.axis_size(axis)
    sums = {}
    for bit in range(0, size, 2):
        near = permute(slots[bit + 1], axis, 1)
        sums[bit] = slots[bit].astype(F32) + near.astype(F32)
    total = sums[0]
    for bit in range(2, size, 2):
        total = total + permute(sums[bit].astype(BF16), axis, bit).astype(F32)
    return total


def reduce_everywhere(whole, scale):
    half = whole.shape[0] // 2
    mine = lax.axis_index("core")
    kept = lax.dynamic_slice_in_dim(whole, mine * half, half, 0)
    sent = lax.dynamic_slice_in_dim(whole, (1 - mine) * half, half, 0)
    kept = kept + permute(sent, "core", 1)
    chips = ("far", "col")
    count = lax.axis_size("far") * lax.axis_size("col")
    parts = lax.all_to_all(kept.astype(BF16).reshape(count, half // count, -1), chips, 0, 0, tiled=True)
    part = (jnp.sum(parts.astype(F32), axis=0) * scale).astype(BF16)
    parts = lax.all_to_all(jnp.broadcast_to(part, (count, *part.shape)), chips, 0, 0, tiled=True)
    kept = parts.reshape(half, -1)
    other = permute(kept, "core", 1)
    whole = jnp.where(mine == 0, jnp.concatenate([kept, other]), jnp.concatenate([other, kept]))
    return whole.astype(F32)


def expand(pair_grad, out_weight, channels, blocks, earlier=()):
    rows, cols, pair_width = pair_grad.shape
    width = channels * rows
    first, count = blocks
    chunk = 8 * channels

    def kernel(*refs):
        grad_ref, weight_ref, *_, expanded_ref, turned_ref, wide = refs
        wide[...] = grad_ref[...].astype(F32).reshape(rows * BLOCK, pair_width)

        def pair_of_columns(step, carry):
            column = step * 2
            for half in range(2):
                turned_ref[column + half] = wide[pl.ds(column + half, rows, stride=BLOCK), :].astype(BF16)
            both = turned_ref[pl.ds(column, 2)].reshape(2 * rows, pair_width)
            for start in range(0, channels * channels, chunk):
                product = lax.dot_general(
                    weight_ref[start : start + chunk, :], both, (((1,), (1,)), ((), ())), preferred_element_type=F32
                ).astype(BF16)
                for half in range(2):
                    row = pl.multiple_of((column + half) * channels, channels)
                    for c1 in range(chunk // channels):
                        expanded_ref[pl.ds(row, channels), pl.ds((start // channels + c1) * rows, rows)] = product[
                            c1 * channels : (c1 + 1) * channels, half * rows : (half + 1) * rows
                        ]
            return carry

        lax.fori_loop(0, BLOCK // 2, pair_of_columns, 0, unroll=2)

    return pl.pallas_call(
        kernel,
        grid=(count,),
        in_specs=[
            pl.BlockSpec((rows, BLOCK, pair_width), lambda b: (0, first + b, 0)),
            pl.BlockSpec(out_weight.shape, lambda b: (0, 0)),
        ]
        + [pl.BlockSpec(memory_space=pl.ANY)] * len(earlier),
        out_specs=[
            pl.BlockSpec((BLOCK * channels, width), lambda b: (first + b, 0)),
            pl.BlockSpec((BLOCK, rows, pair_width), lambda b: (first + b, 0, 0)),
        ],
        out_shape=[
            pltpu.HBM((cols * channels, width), BF16),
            pltpu.HBM((cols, rows, pair_width), BF16),
        ],
        input_output_aliases={2 + n: n for n in range(len(earlier))},
        scratch_shapes=[pltpu.VMEM((rows * BLOCK, pair_width), F32)],
        compiler_params=params(16),
        cost_estimate=cost(
            4 * rows * count * BLOCK * channels * channels * pair_width, 2 * count * BLOCK * channels * width
        ),
        name="expand",
    )(pair_grad, out_weight, *earlier)


def place(pieces, own, target, slot_rows, slot_own):
    rows = pieces[0].shape[0]
    unit = min(rows, slot_rows)
    for bit, piece in enumerate(pieces):
        for part in range(0, rows, unit):
            row = (own ^ bit) * rows + part
            at = ((row // slot_rows) ^ slot_own) * slot_rows + row % slot_rows
            target[pl.ds(pl.multiple_of(at, unit), unit), :] = piece[part : part + unit, :]


def in_hbm(array):
    return pltpu.with_memory_space_constraint(array, pltpu.HBM)


def whole_spec(array):
    return pl.BlockSpec(array.shape, lambda n: (0,) * array.ndim, pipeline_mode=pl.Buffered(1))


def left_product(own, pieces, expanded, slots):
    sequences = pieces[0].shape[0] * len(pieces)
    depth, width = expanded.shape
    tile = 1024

    def kernel(own_ref, *refs):
        piece_refs, expanded_ref = refs[: len(pieces)], refs[len(pieces)]
        outs, panel = refs[len(pieces) + 1 : -1], refs[-1]
        rows = outs[0].shape[0]

        @pl.when(pl.program_id(0) == 0)
        def _():
            place(piece_refs, own_ref[0], panel, rows, own_ref[1])

        product = jnp.dot(panel[...], expanded_ref[...], preferred_element_type=F32)
        for slot, out in enumerate(outs):
            out[...] = product[slot * rows : (slot + 1) * rows, :].astype(out.dtype)

    return pl.pallas_call(
        kernel,
        grid=(width // tile,),
        in_specs=[pl.BlockSpec(memory_space=pltpu.SMEM)]
        + [whole_spec(piece) for piece in pieces]
        + [pl.BlockSpec((depth, tile), lambda n: (0, n))],
        out_specs=[pl.BlockSpec((sequences // slots, tile), lambda n: (0, n))] * slots,
        out_shape=[pltpu.HBM((sequences // slots, width), BF16)] * slots,
        scratch_shapes=[pltpu.VMEM((sequences, depth), BF16)],
        compiler_params=params(18),
        cost_estimate=cost(2 * sequences * depth * width, 2 * depth * width),
        name="left",
    )(own, *pieces, in_hbm(expanded))


def right_product(own, pieces, expanded, slots, after):
    sequences = pieces[0].shape[0] * len(pieces)
    depth, width = expanded.shape
    tile = 512

    def kernel(own_ref, *refs):
        piece_refs, expanded_ref = refs[: len(pieces)], refs[len(pieces)]
        outs, panel = refs[len(pieces) + 2 : -1], refs[-1]
        rows = outs[0].shape[0]

        @pl.when(pl.program_id(0) == 0)
        def _():
            place(piece_refs, own_ref[0], panel, rows, own_ref[1])

        product = lax.dot_general(
            panel[...], expanded_ref[...], (((1,), (1,)), ((), ())), preferred_element_type=F32
        )
        for slot, out in enumerate(outs):
            out[...] = product[slot * rows : (slot + 1) * rows, :].astype(out.dtype)

    return pl.pallas_call(
        kernel,
        grid=(depth // tile,),
        in_specs=[pl.BlockSpec(memory_space=pltpu.SMEM)]
        + [whole_spec(piece) for piece in pieces]
        + [pl.BlockSpec((tile, width), lambda n: (n, 0)), pl.BlockSpec(memory_space=pl.ANY)],
        out_specs=[pl.BlockSpec((sequences // slots, tile), lambda n: (0, n))] * slots,
        out_shape=[pltpu.HBM((sequences // slots, depth), BF16)] * slots,
        scratch_shapes=[pltpu.VMEM((sequences, width), BF16)],
        compiler_params=params(18),
        cost_estimate=cost(2 * sequences * depth * width, 2 * depth * width),
        name="right",
    )(own, *pieces, in_hbm(expanded), after)


def weight_product(own, lefts, rights, turned, channels, after, blocks, earlier=()):
    first, count = blocks
    _, rows, pair_width = turned.shape
    width = lefts[0].shape[1]
    sequences = lefts[0].shape[0] * len(lefts)

    def kernel(own_ref, *refs):
        left_refs, right_refs = refs[: len(lefts)], refs[len(lefts) : len(lefts) + len(rights)]
        turned_ref, _, *earlier_refs = refs[len(lefts) + len(rights) : -5]
        out_ref, left, right, right_t, outer = refs[-5:]
        step = pl.program_id(0)

        @pl.when(step == 0)
        def _():
            place(left_refs, own_ref[1], left, sequences, 0)

        place(right_refs, own_ref[0], right, sequences, 0)
        right_t[...] = right[...].T
        for c1 in range(0, channels, 2):
            product = jnp.dot(
                right_t[...], left[:, c1 * rows : (c1 + 2) * rows], preferred_element_type=F32
            ).astype(BF16)
            for half in range(2):
                for j in range(BLOCK):
                    outer[pl.ds((c1 + half) * channels, channels), pl.ds(j * rows, rows)] = product[
                        j * channels : (j + 1) * channels, half * rows : (half + 1) * rows
                    ]
        total = jnp.dot(
            outer[...], turned_ref[...].reshape(BLOCK * rows, pair_width), preferred_element_type=F32
        )

        @pl.when(step == 0)
        def _():
            out_ref[...] = total + earlier_refs[0][...] if earlier else total

        @pl.when(step != 0)
        def _():
            out_ref[...] += total

    block = BLOCK * channels
    return pl.pallas_call(
        kernel,
        grid=(count,),
        in_specs=[pl.BlockSpec(memory_space=pltpu.SMEM)]
        + [whole_spec(piece) for piece in lefts]
        + [pl.BlockSpec((piece.shape[0], block), lambda b: (0, first + b)) for piece in rights]
        + [pl.BlockSpec((BLOCK, rows, pair_width), lambda b: (first + b, 0, 0)), pl.BlockSpec(memory_space=pl.ANY)]
        + [whole_spec(array) for array in earlier],
        out_specs=pl.BlockSpec((channels * channels, pair_width), lambda b: (0, 0)),
        out_shape=jax.ShapeDtypeStruct((channels * channels, pair_width), F32),
        scratch_shapes=[
            pltpu.VMEM((sequences, width), BF16),
            pltpu.VMEM((sequences, block), BF16),
            pltpu.VMEM((block, sequences), BF16),
            pltpu.VMEM((channels * channels, BLOCK * rows), BF16),
        ],
        compiler_params=params(18),
        cost_estimate=cost(6 * sequences * count * BLOCK * channels * width, 2 * sequences * width),
        name="weight",
    )(own, *lefts, *rights, turned, after, *earlier)


def by_tiles(left_panel, right_panel, pair_grad, out_weight):
    return tile_plan(left_panel, right_panel, pair_grad, out_weight)


def tile_plan(left_panel, right_panel, pair_grad, out_weight):
    left_here, rows, channels = left_panel.shape
    right_here, cols, _ = right_panel.shape
    split_row = ("far", "core")
    own = jnp.stack([lax.axis_index(split_row), lax.axis_index("col")]).astype(jnp.int32)
    left_flat = left_panel.transpose(0, 2, 1).reshape(left_here, channels * rows)
    right_flat = right_panel.reshape(right_here, cols * channels)
    lefts = gather(left_flat, "col")
    rights = gather(right_flat, split_row)
    sequences = left_here * len(lefts)
    scale = 1.0 / sequences

    lefts, rights = [in_hbm(piece) for piece in lefts], [in_hbm(piece) for piece in rights]
    pair_grad, out_weight = in_hbm(pair_grad), in_hbm(out_weight)
    blocks = cols // BLOCK
    early = blocks // 2
    arrays = ()
    if early:
        arrays = expand(pair_grad, out_weight, channels, (0, early))
    expanded, turned = expand(pair_grad, out_weight, channels, (early, blocks - early), arrays)
    left_slots = left_product(own, rights, expanded, len(lefts))
    weight_terms, after = (), left_slots[0]
    for part in ((0, early), (early, blocks - early)):
        if part[1]:
            after = weight_product(own, lefts, rights, turned, channels, after, part, weight_terms)
            weight_terms = (after,)
    weight_terms = after
    right_slots = right_product(own[::-1], lefts, expanded, len(rights), weight_terms)

    left_grad = scatter(left_slots, "col") * scale
    left_grad = left_grad.reshape(left_here, channels, rows).transpose(0, 2, 1)
    right_grad = scatter(right_slots, split_row) * scale
    right_grad = right_grad.reshape(right_here, cols, channels)
    residues = rows * lax.axis_size(split_row)
    weight_grad = reduce_everywhere(weight_terms, scale / residues)
    return left_grad, right_grad, weight_grad


def by_blocks(left_panel, right_panel, pair_grad, out_weight):
    whole_left = lax.all_gather(left_panel, "col", axis=0, tiled=True)
    whole_right = lax.all_gather(right_panel, "row", axis=0, tiled=True)
    sequences, rows_here, channels = whole_left.shape
    cols_here = whole_right.shape[1]
    pair_width = pair_grad.shape[2]
    residues = rows_here * lax.axis_size("row")
    block_rows = 16
    blocks_total = rows_here // block_rows
    right_flat = whole_right.reshape(sequences, cols_here * channels)
    weight_t = out_weight.T

    def advance(carried, block_index):
        right_acc, weight_acc = carried
        first_row = block_index * block_rows
        grad_rows = lax.dynamic_slice_in_dim(pair_grad, first_row, block_rows, 0).reshape(
            block_rows * cols_here, pair_width
        )
        left_rows = lax.dynamic_slice_in_dim(whole_left, first_row, block_rows, 1).reshape(
            sequences, block_rows * channels
        )
        expanded = (
            jnp.dot(grad_rows, weight_t, preferred_element_type=jnp.float32) / sequences
        ).astype(jnp.bfloat16)
        expanded = (
            expanded.reshape(block_rows, cols_here, channels, channels)
            .transpose(0, 2, 1, 3)
            .reshape(block_rows * channels, cols_here * channels)
        )
        left_term = lax.dot_general(
            right_flat, expanded, (((1,), (1,)), ((), ())), preferred_element_type=jnp.float32
        )
        right_acc = right_acc + jnp.dot(left_rows, expanded, preferred_element_type=jnp.float32)
        outer_prod = lax.dot_general(
            left_rows, right_flat, (((0,), (0,)), ((), ())), preferred_element_type=jnp.float32
        )
        outer_prod = (outer_prod / sequences).astype(jnp.bfloat16)
        outer_prod = (
            outer_prod.reshape(block_rows, channels, cols_here, channels)
            .transpose(0, 2, 1, 3)
            .reshape(block_rows * cols_here, channels * channels)
        )
        weight_acc = weight_acc + lax.dot_general(
            outer_prod, grad_rows, (((0,), (0,)), ((), ())), preferred_element_type=jnp.float32
        )
        return ((right_acc, weight_acc), left_term)

    start_state = (
        jnp.zeros((sequences, cols_here * channels), jnp.float32),
        jnp.zeros(out_weight.shape, jnp.float32),
    )
    (right_acc, weight_acc), left_terms = lax.scan(
        advance, start_state, jnp.arange(blocks_total, dtype=jnp.int32)
    )
    left_terms = lax.psum_scatter(left_terms, "col", scatter_dimension=1, tiled=True)
    left_grad = (
        left_terms.reshape(blocks_total, -1, block_rows, channels)
        .transpose(1, 0, 2, 3)
        .reshape(-1, rows_here, channels)
    )
    right_grad = lax.psum_scatter(right_acc, "row", scatter_dimension=0, tiled=True).reshape(
        -1, cols_here, channels
    )
    weight_total = lax.psum(lax.psum(weight_acc, "col"), "row")
    return (left_grad, right_grad, weight_total / residues)


def powers_of_two(*sizes):
    return all(size > 1 and size & (size - 1) == 0 for size in sizes)


def solution(mesh):
    def run(left_panel, right_panel, pair_grad, out_weight):
        n_row, n_col = mesh.shape["row"], mesh.shape["col"]
        rows, cols = pair_grad.shape[0] // n_row, pair_grad.shape[1] // n_col
        tiles = rows == LANES and cols % BLOCK == 0 and powers_of_two(n_row, n_col)
        if tiles:
            devices = mesh.devices.reshape(n_row // 2, 2, n_col)
            used, row, body = Mesh(devices, ("far", "core", "col")), ("far", "core"), by_tiles
        else:
            used, row, body = mesh, "row", by_blocks
        return jax.shard_map(
            body,
            mesh=used,
            in_specs=(P("col", row, None), P(row, "col", None), P(row, "col", None), P()),
            out_specs=(P("col", row, None), P(row, "col", None), P()),
            check_vma=False,
        )(left_panel, right_panel, pair_grad, out_weight)

    return run
```
